1024 devices in a mesh: seq: 16 (over x, y), grp: 64 (over z, core).
Axes of the slice: x: 4, y: 4, z: 32, core: 2. Of those that a mesh axis runs over, the one named last changes fastest.
Arguments:
- p_x: bfloat16 [64, 4096, 2048], P('grp', 'seq'), may hold values from -6 to 6
- p_bc: bfloat16 [64, 4096, 256], P('grp', 'seq'), may hold values from -4 to 4
- p_dt: float32 [64, 32, 4096], P('grp', None, 'seq'), may hold values from 0.005 to 0.04
- p_decay: float32 [64, 32, 4096], P('grp', None, 'seq'), may hold values from -1 to 0
- r_x: bfloat16 [131072, 2048], P('grp', 'seq'), may hold values from -6 to 6
- r_bc: bfloat16 [131072, 256], P('grp'), may hold values from -4 to 4
- r_dt: float32 [32, 131072], P('seq', 'grp'), may hold values from 0.005 to 0.04
- r_decay: float32 [32, 131072], P('seq', 'grp'), may hold values from -1 to 0
- pack_list: int32 [64, 8], P('grp'), may hold values from -1 to 383, as said below
- resp_len: int32 [384], replicated, may hold values from 32 to 256, as said below
- resp_prompt: int32 [384], replicated, may hold values from 0 to 63, as said below
- d_skip: float32 [32], replicated, may hold values from 0.5 to 1.5
Outputs:
- p_out: bfloat16 [64, 4096, 2048], P('grp', 'seq')
- r_out: bfloat16 [131072, 2048], P('grp', 'seq')
The draws below stay inside these ranges and needn't reach their ends.
Inputs may be any that keep to these rules, and one draw needn't show every extreme that they name: `pack_list`: row g lists the responses placed on index g of grp in the order of their rows, -1 marking an empty slot; every response stands in exactly one slot. `resp_len`: a device's responses take its rows one after another from its first row in slot order; the rows after them are unused. `resp_prompt`: every prompt has exactly 6 responses.
All inputs are finite; a program needn't handle non-finite values.
Results may differ from the reference program's by a relative error of at most 0.0053.
Values may be sent and summed in bfloat16 or wider, within the bound.
No kernel may reach another device: no remote copies, remote signals or barrier semaphores. Data moves between devices by JAX's collectives and lax.ppermute only.
A program may use at most 64 MiB of HBM per device.

```python
import math
import jax
import jax.numpy as jnp
from jax import lax

H = 32
P_SIZE = 64
N = 128
STRETCH = 256
SLOTS = 8
RPP = 6
LMAX = 256
LMIN = 32
PROMPTS = 64
PLEN = 4096
RR = 2048
RTOT = 131072
RESP = 384


def decay_rates(key, head_count):
    lowest, highest = (1e-06, 0.06)
    fraction = jax.random.uniform(jax.random.fold_in(key, 7), (head_count,), jnp.float32)
    return jnp.exp(jnp.log(lowest) + fraction * (jnp.log(highest) - jnp.log(lowest)))


def decay_values(key, salt_value, rates_per_head, output_shape, sequence_length):
    noise_key = jax.random.fold_in(key, salt_value)
    first_key, key_second, key_third = jax.random.split(noise_key, 3)
    coarse_rate = jnp.exp(jax.random.uniform(first_key, output_shape, jnp.float32, jnp.log(0.5), jnp.log(2.0)))
    flurry_groups = (jax.random.uniform(key_second, output_shape, jnp.float32) < 2.0 / sequence_length).astype(jnp.float32)
    flurry_size = jax.random.uniform(key_third, output_shape, jnp.float32, 0.22, 0.5)
    return -rates_per_head * coarse_rate - flurry_groups * flurry_size


def draw_p_decay(key, part):
    rates_per_head = decay_rates(key, H)[None, :, None]
    return decay_values(key, 11, rates_per_head, (PROMPTS, H, PLEN), PLEN)


def draw_r_decay(key, part):
    rates_per_head = decay_rates(key, H)[:, None]
    return decay_values(key, 13, rates_per_head, (H, RTOT), PLEN)


def draw_pack_list(key, part):
    slot_order = jax.random.permutation(jax.random.fold_in(key, 21), PROMPTS * SLOTS)
    slot_table = jnp.full((PROMPTS * SLOTS,), -1, jnp.int32).at[slot_order[:RESP]].set(jnp.arange(RESP, dtype=jnp.int32))
    return slot_table.reshape(PROMPTS, SLOTS)


def draw_resp_len(key, part):
    spans = jax.random.randint(jax.random.fold_in(key, 23), (RESP,), LMIN, LMAX + 1, jnp.int32)
    chosen = jax.random.randint(jax.random.fold_in(key, 29), (), 0, RESP, jnp.int32)
    return spans.at[chosen].set(LMAX).astype(jnp.int32)


def draw_resp_prompt(key, part):
    return (jax.random.permutation(jax.random.fold_in(key, 31), RESP) // RPP).astype(jnp.int32)


def block_scale(key, shape, shards, low, high):
    def one(dim, parts):
        heights = jax.random.uniform(jax.random.fold_in(jax.random.fold_in(key, 6), dim), (parts,), jnp.float32, low / len(shards), high / len(shards))
        return jnp.repeat(jnp.exp(heights), shape[dim] // parts).reshape((-1,) + (1,) * (len(shape) - dim - 1))

    level = one(*shards[0])
    for cut in shards[1:]:
        level = level * one(*cut)
    return level


def gaussian(key, extent, width, most, shards=(), held_as=jnp.bfloat16):
    level = block_scale(key, extent, shards, -0.22, 0.18) if shards else 1.0
    result = jax.random.normal(key, extent, jnp.float32) * width * level
    return jnp.minimum(jnp.maximum(result, -most), most).astype(held_as)


def setup_inputs(seed: int = 0) -> dict:
    arg_keys = jax.random.split(jax.random.key(seed), 13)
    p_x = gaussian(arg_keys[0], (PROMPTS, PLEN, H * P_SIZE), 1.0, 6.0, ((0, 64), (1, 16)))
    p_bc = gaussian(arg_keys[1], (PROMPTS, PLEN, 2 * N), (0.3 * (128 / N) ** 0.5), 4.0, ((0, 64), (1, 16)))
    p_dt = jnp.clip(jnp.exp(math.log(0.04) - 2.0794415 * jax.random.uniform(arg_keys[2], (PROMPTS, H, PLEN), jnp.float32) ** block_scale(arg_keys[2], (PROMPTS, H, PLEN), ((0, 64), (2, 16)), -0.2, 0.2)), 0.005, 0.04)
    p_decay = draw_p_decay(jax.random.fold_in(arg_keys[12], 71), 0)
    r_x = gaussian(arg_keys[4], (RTOT, H * P_SIZE), 1.0, 6.0, ((0, 64), (1, 16)))
    r_bc = gaussian(arg_keys[5], (RTOT, 2 * N), (0.3 * (128 / N) ** 0.5), 4.0, ((0, 64),))
    r_dt = jnp.clip(jnp.exp(math.log(0.04) - 2.0794415 * jax.random.uniform(arg_keys[6], (H, RTOT), jnp.float32) ** block_scale(arg_keys[6], (H, RTOT), ((0, 16), (1, 64)), -0.2, 0.2)), 0.005, 0.04)
    r_decay = draw_r_decay(jax.random.fold_in(arg_keys[12], 71), 0)
    pack_list = draw_pack_list(jax.random.fold_in(arg_keys[12], 71), 0)
    resp_len = draw_resp_len(jax.random.fold_in(arg_keys[12], 71), 0)
    resp_prompt = draw_resp_prompt(jax.random.fold_in(arg_keys[12], 71), 0)
    d_skip = jnp.clip(jax.random.uniform(arg_keys[11], (H,), jnp.float32, 0.5, 1.5), 0.5, 1.5)
    return {"p_x": p_x, "p_bc": p_bc, "p_dt": p_dt, "p_decay": p_decay, "r_x": r_x, "r_bc": r_bc, "r_dt": r_dt, "r_decay": r_decay, "pack_list": pack_list, "resp_len": resp_len, "resp_prompt": resp_prompt, "d_skip": d_skip}


def product(einsum_form, left_side, right_side):
    left_side, right_side = lax.optimization_barrier((left_side, right_side))
    return jnp.einsum(einsum_form, left_side.astype(jnp.float32), right_side.astype(jnp.float32))


def block_terms(block_x, block_bc, block_dt, block_decay, block_slot):
    length = block_x.shape[0]
    head_count = block_dt.shape[0]
    state_width = block_bc.shape[1] // 2
    inputs = block_x.reshape(length, head_count, -1)
    b_rows = block_bc[:, :state_width]
    c_rows = block_bc[:, state_width:]
    running = jnp.cumsum(block_decay, axis=1)
    before = running - block_decay
    places = jnp.arange(length)
    same_span = (block_slot[:, None] == block_slot[None, :]) & (places[None, :] <= places[:, None])
    starts_here = jnp.concatenate([jnp.ones((1,), jnp.bool_), block_slot[1:] != block_slot[:-1]])
    leader = same_span & starts_here[None, :]
    offset = jnp.sum(jnp.where(leader[None], before[:, None, :], 0.0), axis=2)
    gained = running - offset
    scores = jnp.dot(c_rows, b_rows.T, preferred_element_type=jnp.float32)
    spread = jnp.where(same_span[None], running[:, :, None] - running[:, None, :], -jnp.inf)
    mixing = (jnp.exp(spread) * block_dt[:, None, :] * scores[None]).astype(jnp.bfloat16)
    inner_part = product("hij,jhp->ihp", mixing, inputs)
    tail_rows = block_slot == block_slot[length - 1]
    to_end = jnp.where(tail_rows[None], jnp.exp(running[:, length - 1:] - running) * block_dt, 0.0)
    scaled = (to_end[:, :, None] * b_rows[None].astype(jnp.float32)).astype(jnp.bfloat16)
    local_state = product("hjn,jhp->hnp", scaled, inputs)
    return inputs, inner_part, gained, local_state, c_rows


def prompt_layer(skip_gain, whole_x, whole_bc, whole_dt, whole_decay):
    blocks = whole_x.shape[0] // STRETCH
    head_count = whole_dt.shape[0]
    state_width = whole_bc.shape[1] // 2
    sliced = (whole_x.reshape(blocks, STRETCH, -1), whole_bc.reshape(blocks, STRETCH, -1),
              whole_dt.reshape(head_count, blocks, STRETCH).transpose(1, 0, 2),
              whole_decay.reshape(head_count, blocks, STRETCH).transpose(1, 0, 2))

    def advance(carried_state, pieces):
        inputs, inner_part, gained, local_state, c_rows = block_terms(pieces[0], pieces[1], pieces[2], pieces[3], jnp.zeros((STRETCH,), jnp.int32))
        carried = product("in,hnp->ihp", c_rows, carried_state.astype(jnp.bfloat16)) * jnp.exp(gained).T[:, :, None]
        output = inner_part + carried + skip_gain[None, :, None] * inputs.astype(jnp.float32)
        carried_state = jnp.exp(gained[:, -1])[:, None, None] * carried_state + local_state
        return carried_state, output.reshape(STRETCH, -1).astype(jnp.bfloat16)

    initial = jnp.zeros((head_count, state_width, whole_x.shape[1] // head_count), jnp.float32)
    final_state, outputs = lax.scan(advance, initial, sliced)
    return outputs.reshape(whole_x.shape), final_state.astype(jnp.bfloat16)


def response_layer(skip_gain, rows_x, rows_bc, rows_dt, rows_decay, row_slot, slot_seeds):
    slot_count = slot_seeds.shape[0]
    blocks = rows_x.shape[0] // STRETCH
    head_count = rows_dt.shape[0]
    sliced = (rows_x.reshape(blocks, STRETCH, -1), rows_bc.reshape(blocks, STRETCH, -1),
              rows_dt.reshape(head_count, blocks, STRETCH).transpose(1, 0, 2),
              rows_decay.reshape(head_count, blocks, STRETCH).transpose(1, 0, 2),
              row_slot.reshape(blocks, STRETCH))
    slot_ids = jnp.arange(slot_count)

    def advance(carry_pair, pieces):
        carried_state, previous = carry_pair
        block_slot = pieces[4]
        inputs, inner_part, gained, local_state, c_rows = block_terms(pieces[0], pieces[1], pieces[2], pieces[3], block_slot)
        first_slot = block_slot[0]
        carried_on = first_slot == previous
        chosen = (slot_ids == first_slot) & carried_on
        bases_table = jnp.where(chosen[:, None, None, None], carried_state.astype(jnp.bfloat16)[None], slot_seeds)
        projected = product("in,khnp->ikhp", c_rows, bases_table)
        hot_rows = (block_slot[:, None] == slot_ids[None, :]).astype(jnp.float32)
        carried = jnp.sum(projected * hot_rows[:, :, None, None], axis=1) * jnp.exp(gained).T[:, :, None]
        output = inner_part + carried + skip_gain[None, :, None] * inputs.astype(jnp.float32)
        output = jnp.where((block_slot < slot_count)[:, None, None], output, 0.0)
        final_slot = block_slot[STRETCH - 1]
        fresh_seed = jnp.sum(jnp.where((slot_ids == final_slot)[:, None, None, None], slot_seeds.astype(jnp.float32), 0.0), axis=0)
        anchor = jnp.where((final_slot == first_slot) & carried_on, carried_state, fresh_seed)
        carried_state = jnp.exp(gained[:, -1])[:, None, None] * anchor + local_state
        return (carried_state, final_slot), output.reshape(STRETCH, -1).astype(jnp.bfloat16)

    initial = (jnp.zeros(slot_seeds.shape[1:], jnp.float32), jnp.int32(-1))
    final_pair, outputs = lax.scan(advance, initial, sliced)
    return outputs.reshape(rows_x.shape)


def slot_layout(pack_row, resp_len, resp_prompt, row_count):
    hit_table = pack_row[:, None] == jnp.arange(resp_len.shape[0])[None, :]
    slot_spans = jnp.sum(jnp.where(hit_table, resp_len[None, :], 0), axis=1).astype(jnp.int32)
    owners = jnp.where(pack_row >= 0, jnp.sum(jnp.where(hit_table, resp_prompt[None, :], 0), axis=1), -1)
    limits = jnp.cumsum(slot_spans)
    row_slot = jnp.sum((jnp.arange(row_count)[:, None] >= limits[None, :]).astype(jnp.int32), axis=1)
    return row_slot.astype(jnp.int32), owners.astype(jnp.int32)


def reference(p_x, p_bc, p_dt, p_decay, r_x, r_bc, r_dt, r_decay, pack_list, resp_len, resp_prompt, d_skip):
    def one_prompt(element):
        return prompt_layer(d_skip, element[0], element[1], element[2], element[3])

    p_out, seeds_all = lax.map(one_prompt, (p_x, p_bc, p_dt, p_decay))
    head_count = r_dt.shape[0]
    rows_dt = r_dt.reshape(head_count, PROMPTS, RR).transpose(1, 0, 2)
    rows_decay = r_decay.reshape(head_count, PROMPTS, RR).transpose(1, 0, 2)

    def one_device(element):
        row_slot, owners = slot_layout(element[4], resp_len, resp_prompt, RR)
        pick_table = (owners[:, None] == jnp.arange(PROMPTS)[None, :]).astype(jnp.float32)
        slot_seeds = product("kq,qhnp->khnp", pick_table, seeds_all).astype(jnp.bfloat16)
        return response_layer(d_skip, element[0], element[1], element[2], element[3], row_slot, slot_seeds)

    r_out = lax.map(one_device, (r_x.reshape(PROMPTS, RR, -1), r_bc.reshape(PROMPTS, RR, -1), rows_dt, rows_decay, pack_list))
    return p_out, r_out.reshape(r_x.shape)
```

```python
import jax
import jax.numpy as jnp
from jax import lax
from jax.sharding import PartitionSpec as P

STRETCH = 256


def product(einsum_form, left_side, right_side):
    return jnp.einsum(einsum_form, left_side, right_side, preferred_element_type=jnp.float32)


def block_terms(block_x, block_bc, block_dt, block_decay, block_slot):
    length = block_x.shape[0]
    head_count = block_dt.shape[0]
    state_width = block_bc.shape[1] // 2
    inputs = block_x.reshape(length, head_count, -1)
    b_rows = block_bc[:, :state_width]
    c_rows = block_bc[:, state_width:]
    running = jnp.cumsum(block_decay, axis=1)
    before = running - block_decay
    places = jnp.arange(length)
    same_span = (block_slot[:, None] == block_slot[None, :]) & (places[None, :] <= places[:, None])
    starts_here = jnp.concatenate([jnp.ones((1,), jnp.bool_), block_slot[1:] != block_slot[:-1]])
    leader = same_span & starts_here[None, :]
    offset = jnp.sum(jnp.where(leader[None], before[:, None, :], 0.0), axis=2)
    gained = running - offset
    scores = jnp.dot(c_rows, b_rows.T, preferred_element_type=jnp.float32)
    spread = jnp.where(same_span[None], running[:, :, None] - running[:, None, :], -jnp.inf)
    mixing = (jnp.exp(spread) * block_dt[:, None, :] * scores[None]).astype(jnp.bfloat16)
    inner_part = product("hij,jhp->ihp", mixing, inputs)
    tail_rows = block_slot == block_slot[length - 1]
    to_end = jnp.where(tail_rows[None], jnp.exp(running[:, length - 1 :] - running) * block_dt, 0.0)
    scaled = (to_end[:, :, None] * b_rows[None].astype(jnp.float32)).astype(jnp.bfloat16)
    local_state = product("hjn,jhp->hnp", scaled, inputs)
    return (inputs, inner_part, gained, local_state, c_rows)


def slot_layout(pack_row, resp_len, resp_prompt, row_count):
    hit_table = pack_row[:, None] == jnp.arange(resp_len.shape[0])[None, :]
    slot_spans = jnp.sum(jnp.where(hit_table, resp_len[None, :], 0), axis=1)
    owners = jnp.where(
        pack_row >= 0, jnp.sum(jnp.where(hit_table, resp_prompt[None, :], 0), axis=1), -1
    )
    limits = jnp.cumsum(slot_spans)
    row_slot = jnp.sum(
        (jnp.arange(row_count)[:, None] >= limits[None, :]).astype(jnp.int32), axis=1
    )
    return (row_slot, owners)


def prompt_part(p_x, p_bc, p_dt, p_decay, d_skip):
    head_count = p_dt.shape[1]
    groups = lax.axis_size("seq")
    block_heads = head_count // groups
    state_width = p_bc.shape[2] // 2
    inputs, inner_part, gained, local_state, c_rows = block_terms(
        p_x[0], p_bc[0], p_dt[0], p_decay[0], jnp.zeros((STRETCH,), jnp.int32)
    )
    channels = inputs.shape[2]
    block_gain = jnp.exp(gained[:, -1])
    pad = 8
    gain_rows = jnp.broadcast_to(block_gain[:, None, None], (head_count, pad, channels))
    payload = jnp.concatenate([local_state, gain_rows], axis=1)
    payload = payload.reshape(groups, block_heads, state_width + pad, channels)
    arrived = lax.all_to_all(payload, "seq", 0, 0, tiled=True)
    pieces = arrived[:, :, :state_width, :]
    gains = arrived[:, :, state_width, 0]
    state = jnp.zeros((block_heads, state_width, channels), jnp.float32)
    prefixes = []
    for position in range(groups):
        prefixes.append(state.astype(jnp.bfloat16))
        state = gains[position][:, None, None] * state + pieces[position]
    own_seed = state.astype(jnp.bfloat16)
    sent_back = jnp.stack(prefixes, axis=0)
    prefix = lax.all_to_all(sent_back, "seq", 0, 0, tiled=True)
    prefix = prefix.reshape(head_count, state_width, channels)
    carried = product("in,hnp->ihp", c_rows, prefix) * jnp.exp(gained).T[:, :, None]
    output = inner_part + carried + d_skip[None, :, None] * inputs.astype(jnp.float32)
    p_out = output.reshape(STRETCH, -1).astype(jnp.bfloat16)[None]
    return p_out, own_seed


def response_part(skip_gain, rows_x, rows_bc, rows_dt, rows_decay, row_slot, slot_seeds):
    slot_count = slot_seeds.shape[0]
    blocks = rows_x.shape[0] // STRETCH
    head_count = rows_dt.shape[0]
    state_width = rows_bc.shape[1] // 2
    sliced = (
        rows_x.reshape(blocks, STRETCH, -1),
        rows_bc.reshape(blocks, STRETCH, -1),
        rows_dt.reshape(head_count, blocks, STRETCH).transpose(1, 0, 2),
        rows_decay.reshape(head_count, blocks, STRETCH).transpose(1, 0, 2),
        row_slot.reshape(blocks, STRETCH),
    )
    inputs, inner_part, gained, local_state, c_rows = jax.vmap(block_terms)(*sliced)
    block_slot = sliced[4]
    channels = inputs.shape[3]
    slot_ids = jnp.arange(slot_count)
    seeds_f32 = slot_seeds.astype(jnp.float32)
    block_gain = jnp.exp(gained[:, :, -1])

    state = jnp.zeros((head_count, state_width, channels), jnp.float32)
    previous = jnp.int32(-1)
    continued_bases = []
    continued_flags = []
    for block in range(blocks):
        first_slot = block_slot[block, 0]
        final_slot = block_slot[block, STRETCH - 1]
        carried_on = first_slot == previous
        continued_bases.append(state.astype(jnp.bfloat16))
        continued_flags.append(carried_on)
        fresh_seed = jnp.sum(
            jnp.where((slot_ids == final_slot)[:, None, None, None], seeds_f32, 0.0), axis=0
        )
        anchor = jnp.where((final_slot == first_slot) & carried_on, state, fresh_seed)
        state = block_gain[block][:, None, None] * anchor + local_state[block]
        previous = final_slot
    continued_bases = jnp.stack(continued_bases, axis=0)
    continued_flags = jnp.stack(continued_flags, axis=0)

    hot_rows = (block_slot[:, :, None] == slot_ids[None, None, :]).astype(jnp.bfloat16)
    masked_c = (c_rows[:, :, None, :] * hot_rows[:, :, :, None]).reshape(
        blocks * STRETCH, slot_count * state_width
    )
    seed_table = slot_seeds.transpose(0, 2, 1, 3).reshape(
        slot_count * state_width, head_count * channels
    )
    from_seeds = jnp.dot(masked_c, seed_table, preferred_element_type=jnp.float32)
    from_seeds = from_seeds.reshape(blocks, STRETCH, head_count, channels)
    from_state = product("bin,bhnp->bihp", c_rows, continued_bases)
    continues_row = continued_flags[:, None] & (block_slot == block_slot[:, :1])
    projected = jnp.where(continues_row[:, :, None, None], from_state, from_seeds)
    carried = projected * jnp.exp(gained).transpose(0, 2, 1)[:, :, :, None]
    output = inner_part + carried + skip_gain[None, None, :, None] * inputs.astype(jnp.float32)
    output = jnp.where((block_slot < slot_count)[:, :, None, None], output, 0.0)
    return output.reshape(rows_x.shape).astype(jnp.bfloat16)


def on_device(
    p_x, p_bc, p_dt, p_decay, r_x, r_bc, r_dt, r_decay, pack_list, resp_len, resp_prompt, d_skip
):
    head_count = p_dt.shape[1]
    groups = lax.axis_size("seq")
    block_heads = head_count // groups
    p_out, own_seed = prompt_part(p_x, p_bc, p_dt, p_decay, d_skip)
    row_slot, owners = slot_layout(pack_list[0], resp_len, resp_prompt, r_x.shape[0])
    gathered_piece = lax.all_gather(own_seed[None], "grp", axis=0, tiled=True)
    chosen = (owners[:, None] == jnp.arange(gathered_piece.shape[0])[None, :]).astype(jnp.bfloat16)
    slot_seeds = product("km,mhnp->khnp", chosen, gathered_piece).astype(jnp.bfloat16)
    skip_block = lax.dynamic_slice_in_dim(
        d_skip, lax.axis_index("seq") * block_heads, block_heads, 0
    )
    r_out = response_part(skip_block, r_x, r_bc, r_dt, r_decay, row_slot, slot_seeds)
    return (p_out, r_out)


def solution(mesh):
    placed = (
        P("grp", "seq", None),
        P("grp", "seq", None),
        P("grp", None, "seq"),
        P("grp", None, "seq"),
        P("grp", "seq"),
        P("grp", None),
        P("seq", "grp"),
        P("seq", "grp"),
        P("grp", None),
        P(),
        P(),
        P(),
    )
    return jax.shard_map(
        on_device,
        mesh=mesh,
        in_specs=placed,
        out_specs=(P("grp", "seq", None), P("grp", "seq")),
        check_vma=False,
    )
```

```python
import jax
import jax.numpy as jnp
from jax import lax
from jax.sharding import PartitionSpec as P

STRETCH = 256


def product(einsum_form, left_side, right_side):
    return jnp.einsum(einsum_form, left_side, right_side, preferred_element_type=jnp.float32)


def block_terms(block_x, block_bc, block_dt, block_decay, block_slot):
    length = block_x.shape[0]
    head_count = block_dt.shape[0]
    state_width = block_bc.shape[1] // 2
    inputs = block_x.reshape(length, head_count, -1)
    b_rows = block_bc[:, :state_width]
    c_rows = block_bc[:, state_width:]
    running = jnp.cumsum(block_decay, axis=1)
    before = running - block_decay
    places = jnp.arange(length)
    same_span = (block_slot[:, None] == block_slot[None, :]) & (places[None, :] <= places[:, None])
    starts_here = jnp.concatenate([jnp.ones((1,), jnp.bool_), block_slot[1:] != block_slot[:-1]])
    leader = same_span & starts_here[None, :]
    offset = jnp.sum(jnp.where(leader[None], before[:, None, :], 0.0), axis=2)
    gained = running - offset
    scores = jnp.dot(c_rows, b_rows.T, preferred_element_type=jnp.float32)
    spread = jnp.where(same_span[None], running[:, :, None] - running[:, None, :], -jnp.inf)
    mixing = (jnp.exp(spread) * block_dt[:, None, :] * scores[None]).astype(jnp.bfloat16)
    inner_part = product("hij,jhp->ihp", mixing, inputs)
    tail_rows = block_slot == block_slot[length - 1]
    to_end = jnp.where(tail_rows[None], jnp.exp(running[:, length - 1 :] - running) * block_dt, 0.0)
    scaled = (to_end[:, :, None] * b_rows[None].astype(jnp.float32)).astype(jnp.bfloat16)
    local_state = product("hjn,jhp->hnp", scaled, inputs)
    return (inputs, inner_part, gained, local_state, c_rows)


def slot_layout(pack_row, resp_len, resp_prompt, row_count):
    hit_table = pack_row[:, None] == jnp.arange(resp_len.shape[0])[None, :]
    slot_spans = jnp.sum(jnp.where(hit_table, resp_len[None, :], 0), axis=1)
    owners = jnp.where(
        pack_row >= 0, jnp.sum(jnp.where(hit_table, resp_prompt[None, :], 0), axis=1), -1
    )
    limits = jnp.cumsum(slot_spans)
    row_slot = jnp.sum(
        (jnp.arange(row_count)[:, None] >= limits[None, :]).astype(jnp.int32), axis=1
    )
    return (row_slot, owners)


def prompt_part(p_x, p_bc, p_dt, p_decay, d_skip):
    head_count = p_dt.shape[1]
    groups = lax.axis_size("seq")
    block_heads = head_count // groups
    state_width = p_bc.shape[2] // 2
    inputs, inner_part, gained, local_state, c_rows = block_terms(
        p_x[0], p_bc[0], p_dt[0], p_decay[0], jnp.zeros((STRETCH,), jnp.int32)
    )
    channels = inputs.shape[2]
    block_gain = gained[:, -1]
    pad = 8
    gain_rows = jnp.broadcast_to(block_gain[:, None, None], (head_count, pad, channels))
    payload = jnp.concatenate([local_state, gain_rows], axis=1)
    payload = payload.reshape(groups, block_heads, state_width + pad, channels)
    arrived = lax.all_to_all(payload, "seq", 0, 0, tiled=True)
    pieces = arrived[:, :, :state_width, :]
    log_gains = arrived[:, :, state_width, 0]
    ends = jnp.arange(groups + 1)[:, None, None]
    sources = jnp.arange(groups)[None, :, None]
    between = jnp.arange(groups)[None, None, :]
    spans = (sources < between) & (between < ends)
    exponents = jnp.sum(jnp.where(spans[..., None], log_gains[None, None], 0.0), axis=2)
    weights = jnp.where(sources < ends, jnp.exp(exponents), 0.0)
    states = jnp.sum(weights[:, :, :, None, None] * pieces[None], axis=1)
    own_seed = states[groups].astype(jnp.bfloat16)
    sent_back = states[:groups].astype(jnp.bfloat16)
    prefix = lax.all_to_all(sent_back, "seq", 0, 0, tiled=True)
    prefix = prefix.reshape(head_count, state_width, channels)
    carried = product("in,hnp->ihp", c_rows, prefix) * jnp.exp(gained).T[:, :, None]
    output = inner_part + carried + d_skip[None, :, None] * inputs.astype(jnp.float32)
    p_out = output.reshape(STRETCH, -1).astype(jnp.bfloat16)[None]
    return p_out, own_seed


def response_part(skip_gain, rows_x, rows_bc, rows_dt, rows_decay, row_slot, slot_seeds):
    slot_count = slot_seeds.shape[0]
    blocks = rows_x.shape[0] // STRETCH
    head_count = rows_dt.shape[0]
    state_width = rows_bc.shape[1] // 2
    sliced = (
        rows_x.reshape(blocks, STRETCH, -1),
        rows_bc.reshape(blocks, STRETCH, -1),
        rows_dt.reshape(head_count, blocks, STRETCH).transpose(1, 0, 2),
        rows_decay.reshape(head_count, blocks, STRETCH).transpose(1, 0, 2),
        row_slot.reshape(blocks, STRETCH),
    )
    inputs, inner_part, gained, local_state, c_rows = jax.vmap(block_terms)(*sliced)
    block_slot = sliced[4]
    channels = inputs.shape[3]
    slot_ids = jnp.arange(slot_count)
    seeds_f32 = slot_seeds.astype(jnp.float32)
    block_gain = jnp.exp(gained[:, :, -1])

    state = jnp.zeros((head_count, state_width, channels), jnp.float32)
    previous = jnp.int32(-1)
    continued_bases = []
    continued_flags = []
    for block in range(blocks):
        first_slot = block_slot[block, 0]
        final_slot = block_slot[block, STRETCH - 1]
        carried_on = first_slot == previous
        continued_bases.append(state.astype(jnp.bfloat16))
        continued_flags.append(carried_on)
        fresh_seed = jnp.sum(
            jnp.where((slot_ids == final_slot)[:, None, None, None], seeds_f32, 0.0), axis=0
        )
        anchor = jnp.where((final_slot == first_slot) & carried_on, state, fresh_seed)
        state = block_gain[block][:, None, None] * anchor + local_state[block]
        previous = final_slot
    continued_bases = jnp.stack(continued_bases, axis=0)
    continued_flags = jnp.stack(continued_flags, axis=0)

    hot_rows = (block_slot[:, :, None] == slot_ids[None, None, :]).astype(jnp.bfloat16)
    masked_c = (c_rows[:, :, None, :] * hot_rows[:, :, :, None]).reshape(
        blocks * STRETCH, slot_count * state_width
    )
    seed_table = slot_seeds.transpose(0, 2, 1, 3).reshape(
        slot_count * state_width, head_count * channels
    )
    from_seeds = jnp.dot(masked_c, seed_table, preferred_element_type=jnp.float32)
    from_seeds = from_seeds.reshape(blocks, STRETCH, head_count, channels)
    from_state = product("bin,bhnp->bihp", c_rows, continued_bases)
    continues_row = continued_flags[:, None] & (block_slot == block_slot[:, :1])
    projected = jnp.where(continues_row[:, :, None, None], from_state, from_seeds)
    carried = projected * jnp.exp(gained).transpose(0, 2, 1)[:, :, :, None]
    output = inner_part + carried + skip_gain[None, None, :, None] * inputs.astype(jnp.float32)
    output = jnp.where((block_slot < slot_count)[:, :, None, None], output, 0.0)
    return output.reshape(rows_x.shape).astype(jnp.bfloat16)


def on_device(
    p_x, p_bc, p_dt, p_decay, r_x, r_bc, r_dt, r_decay, pack_list, resp_len, resp_prompt, d_skip
):
    head_count = p_dt.shape[1]
    groups = lax.axis_size("seq")
    block_heads = head_count // groups
    p_out, own_seed = prompt_part(p_x, p_bc, p_dt, p_decay, d_skip)
    own_seed, r_x, r_bc, r_dt, r_decay = lax.optimization_barrier(
        (own_seed, r_x, r_bc, r_dt, r_decay)
    )
    row_slot, owners = slot_layout(pack_list[0], resp_len, resp_prompt, r_x.shape[0])
    gathered_piece = lax.all_gather(own_seed[None], "grp", axis=0, tiled=True)
    chosen = (owners[:, None] == jnp.arange(gathered_piece.shape[0])[None, :]).astype(jnp.bfloat16)
    slot_seeds = product("km,mhnp->khnp", chosen, gathered_piece).astype(jnp.bfloat16)
    skip_block = lax.dynamic_slice_in_dim(
        d_skip, lax.axis_index("seq") * block_heads, block_heads, 0
    )
    r_out = response_part(skip_block, r_x, r_bc, r_dt, r_decay, row_slot, slot_seeds)
    return (p_out, r_out)


def solution(mesh):
    placed = (
        P("grp", "seq", None),
        P("grp", "seq", None),
        P("grp", None, "seq"),
        P("grp", None, "seq"),
        P("grp", "seq"),
        P("grp", None),
        P("seq", "grp"),
        P("seq", "grp"),
        P("grp", None),
        P(),
        P(),
        P(),
    )
    return jax.shard_map(
        on_device,
        mesh=mesh,
        in_specs=placed,
        out_specs=(P("grp", "seq", None), P("grp", "seq")),
        check_vma=False,
    )
```

```python
import jax
import jax.numpy as jnp
from jax import lax
from jax.sharding import PartitionSpec as P

STRETCH = 256


def product(einsum_form, left_side, right_side):
    return jnp.einsum(einsum_form, left_side, right_side, preferred_element_type=jnp.float32)


def block_terms(block_x, block_bc, block_dt, block_decay, block_slot):
    length = block_x.shape[0]
    head_count = block_dt.shape[0]
    state_width = block_bc.shape[1] // 2
    inputs = block_x.reshape(length, head_count, -1)
    b_rows = block_bc[:, :state_width]
    c_rows = block_bc[:, state_width:]
    running = jnp.cumsum(block_decay, axis=1)
    before = running - block_decay
    places = jnp.arange(length)
    same_span = (block_slot[:, None] == block_slot[None, :]) & (places[None, :] <= places[:, None])
    starts_here = jnp.concatenate([jnp.ones((1,), jnp.bool_), block_slot[1:] != block_slot[:-1]])
    leader = same_span & starts_here[None, :]
    offset = jnp.sum(jnp.where(leader[None], before[:, None, :], 0.0), axis=2)
    gained = running - offset
    scores = jnp.dot(c_rows, b_rows.T, preferred_element_type=jnp.float32)
    spread = jnp.where(same_span[None], running[:, :, None] - running[:, None, :], -jnp.inf)
    mixing = (jnp.exp(spread) * block_dt[:, None, :] * scores[None]).astype(jnp.bfloat16)
    inner_part = product("hij,jhp->ihp", mixing, inputs)
    tail_rows = block_slot == block_slot[length - 1]
    to_end = jnp.where(tail_rows[None], jnp.exp(running[:, length - 1 :] - running) * block_dt, 0.0)
    scaled = (to_end[:, :, None] * b_rows[None].astype(jnp.float32)).astype(jnp.bfloat16)
    local_state = product("hjn,jhp->hnp", scaled, inputs)
    return (inputs, inner_part, gained, local_state, c_rows)


def slot_layout(pack_row, resp_len, resp_prompt, row_count):
    hit_table = pack_row[:, None] == jnp.arange(resp_len.shape[0])[None, :]
    slot_spans = jnp.sum(jnp.where(hit_table, resp_len[None, :], 0), axis=1)
    owners = jnp.where(
        pack_row >= 0, jnp.sum(jnp.where(hit_table, resp_prompt[None, :], 0), axis=1), -1
    )
    limits = jnp.cumsum(slot_spans)
    row_slot = jnp.sum(
        (jnp.arange(row_count)[:, None] >= limits[None, :]).astype(jnp.int32), axis=1
    )
    return (row_slot, owners)


def prompt_part(p_x, p_bc, p_dt, p_decay, d_skip):
    head_count = p_dt.shape[1]
    groups = lax.axis_size("seq")
    block_heads = head_count // groups
    state_width = p_bc.shape[2] // 2
    inputs, inner_part, gained, local_state, c_rows = block_terms(
        p_x[0], p_bc[0], p_dt[0], p_decay[0], jnp.zeros((STRETCH,), jnp.int32)
    )
    channels = inputs.shape[2]
    block_gain = gained[:, -1]
    pad = 8
    gain_rows = jnp.broadcast_to(block_gain[:, None, None], (head_count, pad, channels))
    payload = jnp.concatenate([local_state, gain_rows], axis=1)
    payload = payload.reshape(groups, block_heads, state_width + pad, channels)
    arrived = lax.all_to_all(payload, "seq", 0, 0, tiled=True)
    pieces = arrived[:, :, :state_width, :]
    log_gains = arrived[:, :, state_width, 0]
    ends = jnp.arange(groups + 1)[:, None, None]
    sources = jnp.arange(groups)[None, :, None]
    between = jnp.arange(groups)[None, None, :]
    spans = (sources < between) & (between < ends)
    exponents = jnp.sum(jnp.where(spans[..., None], log_gains[None, None], 0.0), axis=2)
    weights = jnp.where(sources < ends, jnp.exp(exponents), 0.0)
    states = jnp.sum(weights[:, :, :, None, None] * pieces[None], axis=1)
    own_seed = states[groups].astype(jnp.bfloat16)
    sent_back = states[:groups].astype(jnp.bfloat16)
    prefix = lax.all_to_all(sent_back, "seq", 0, 0, tiled=True)
    prefix = prefix.reshape(head_count, state_width, channels)
    carried = product("in,hnp->ihp", c_rows, prefix) * jnp.exp(gained).T[:, :, None]
    output = inner_part + carried + d_skip[None, :, None] * inputs.astype(jnp.float32)
    p_out = output.reshape(STRETCH, -1).astype(jnp.bfloat16)[None]
    return p_out, own_seed


def response_part(skip_gain, rows_x, rows_bc, rows_dt, rows_decay, row_slot, slot_seeds):
    slot_count = slot_seeds.shape[0]
    blocks = rows_x.shape[0] // STRETCH
    head_count = rows_dt.shape[0]
    state_width = rows_bc.shape[1] // 2
    sliced = (
        rows_x.reshape(blocks, STRETCH, -1),
        rows_bc.reshape(blocks, STRETCH, -1),
        rows_dt.reshape(head_count, blocks, STRETCH).transpose(1, 0, 2),
        rows_decay.reshape(head_count, blocks, STRETCH).transpose(1, 0, 2),
        row_slot.reshape(blocks, STRETCH),
    )
    inputs, inner_part, gained, local_state, c_rows = jax.vmap(block_terms)(*sliced)
    block_slot = sliced[4]
    channels = inputs.shape[3]
    slot_ids = jnp.arange(slot_count)
    seeds_f32 = slot_seeds.astype(jnp.float32)
    block_gain = jnp.exp(gained[:, :, -1])

    state = jnp.zeros((head_count, state_width, channels), jnp.float32)
    previous = jnp.int32(-1)
    continued_bases = []
    continued_flags = []
    for block in range(blocks):
        first_slot = block_slot[block, 0]
        final_slot = block_slot[block, STRETCH - 1]
        carried_on = first_slot == previous
        continued_bases.append(state.astype(jnp.bfloat16))
        continued_flags.append(carried_on)
        fresh_seed = jnp.sum(
            jnp.where((slot_ids == final_slot)[:, None, None, None], seeds_f32, 0.0), axis=0
        )
        anchor = jnp.where((final_slot == first_slot) & carried_on, state, fresh_seed)
        state = block_gain[block][:, None, None] * anchor + local_state[block]
        previous = final_slot
    continued_bases = jnp.stack(continued_bases, axis=0)
    continued_flags = jnp.stack(continued_flags, axis=0)

    hot_rows = (block_slot[:, :, None] == slot_ids[None, None, :]).astype(jnp.bfloat16)
    masked_c = (c_rows[:, :, None, :] * hot_rows[:, :, :, None]).reshape(
        blocks * STRETCH, slot_count * state_width
    )
    seed_table = slot_seeds.transpose(0, 2, 1, 3).reshape(
        slot_count * state_width, head_count * channels
    )
    from_seeds = jnp.dot(masked_c, seed_table, preferred_element_type=jnp.float32)
    from_seeds = from_seeds.reshape(blocks, STRETCH, head_count, channels)
    from_state = product("bin,bhnp->bihp", c_rows, continued_bases)
    continues_row = continued_flags[:, None] & (block_slot == block_slot[:, :1])
    projected = jnp.where(continues_row[:, :, None, None], from_state, from_seeds)
    carried = projected * jnp.exp(gained).transpose(0, 2, 1)[:, :, :, None]
    output = inner_part + carried + skip_gain[None, None, :, None] * inputs.astype(jnp.float32)
    output = jnp.where((block_slot < slot_count)[:, :, None, None], output, 0.0)
    return output.reshape(rows_x.shape).astype(jnp.bfloat16)


def gather_all(piece, axis):
    count = lax.axis_size(axis)
    mine = lax.axis_index(axis)
    rounds = count.bit_length() - 1
    assert 1 << rounds == count
    held = piece
    for level in range(rounds):
        step = 1 << (rounds - 1 - level)
        pairs = [(index, index ^ step) for index in range(count)]
        other = lax.ppermute(held, axis, pairs)
        lower = (mine & step) == 0
        held = jnp.stack(
            [jnp.where(lower, held, other), jnp.where(lower, other, held)], axis=level
        )
    return held.reshape((count,) + piece.shape)


def on_device(
    p_x, p_bc, p_dt, p_decay, r_x, r_bc, r_dt, r_decay, pack_list, resp_len, resp_prompt, d_skip
):
    head_count = p_dt.shape[1]
    groups = lax.axis_size("seq")
    block_heads = head_count // groups
    p_out, own_seed = prompt_part(p_x, p_bc, p_dt, p_decay, d_skip)
    own_seed, r_x, r_bc, r_dt, r_decay = lax.optimization_barrier(
        (own_seed, r_x, r_bc, r_dt, r_decay)
    )
    row_slot, owners = slot_layout(pack_list[0], resp_len, resp_prompt, r_x.shape[0])
    gathered_piece = gather_all(own_seed, "grp")
    chosen = (owners[:, None] == jnp.arange(gathered_piece.shape[0])[None, :]).astype(jnp.bfloat16)
    slot_seeds = product("km,mhnp->khnp", chosen, gathered_piece).astype(jnp.bfloat16)
    skip_block = lax.dynamic_slice_in_dim(
        d_skip, lax.axis_index("seq") * block_heads, block_heads, 0
    )
    r_out = response_part(skip_block, r_x, r_bc, r_dt, r_decay, row_slot, slot_seeds)
    return (p_out, r_out)


def solution(mesh):
    placed = (
        P("grp", "seq", None),
        P("grp", "seq", None),
        P("grp", None, "seq"),
        P("grp", None, "seq"),
        P("grp", "seq"),
        P("grp", None),
        P("seq", "grp"),
        P("seq", "grp"),
        P("grp", None),
        P(),
        P(),
        P(),
    )
    return jax.shard_map(
        on_device,
        mesh=mesh,
        in_specs=placed,
        out_specs=(P("grp", "seq", None), P("grp", "seq")),
        check_vma=False,
    )
```

```python
import jax
import jax.numpy as jnp
from jax import lax
from jax.sharding import PartitionSpec as P

STRETCH = 256


def product(einsum_form, left_side, right_side):
    return jnp.einsum(einsum_form, left_side, right_side, preferred_element_type=jnp.float32)


def block_terms(block_x, block_bc, block_dt, block_decay, block_slot):
    length = block_x.shape[0]
    head_count = block_dt.shape[0]
    state_width = block_bc.shape[1] // 2
    inputs = block_x.reshape(length, head_count, -1)
    b_rows = block_bc[:, :state_width]
    c_rows = block_bc[:, state_width:]
    running = jnp.cumsum(block_decay, axis=1)
    before = running - block_decay
    places = jnp.arange(length)
    same_span = (block_slot[:, None] == block_slot[None, :]) & (places[None, :] <= places[:, None])
    starts_here = jnp.concatenate([jnp.ones((1,), jnp.bool_), block_slot[1:] != block_slot[:-1]])
    leader = same_span & starts_here[None, :]
    offset = jnp.sum(jnp.where(leader[None], before[:, None, :], 0.0), axis=2)
    gained = running - offset
    scores = jnp.dot(c_rows, b_rows.T, preferred_element_type=jnp.float32)
    spread = jnp.where(same_span[None], running[:, :, None] - running[:, None, :], -jnp.inf)
    mixing = (jnp.exp(spread) * block_dt[:, None, :] * scores[None]).astype(jnp.bfloat16)
    inner_part = product("hij,jhp->ihp", mixing, inputs)
    tail_rows = block_slot == block_slot[length - 1]
    to_end = jnp.where(tail_rows[None], jnp.exp(running[:, length - 1 :] - running) * block_dt, 0.0)
    scaled = (to_end[:, :, None] * b_rows[None].astype(jnp.float32)).astype(jnp.bfloat16)
    local_state = product("hjn,jhp->hnp", scaled, inputs)
    return (inputs, inner_part, gained, local_state, c_rows)


def slot_layout(pack_row, resp_len, resp_prompt, row_count):
    hit_table = pack_row[:, None] == jnp.arange(resp_len.shape[0])[None, :]
    slot_spans = jnp.sum(jnp.where(hit_table, resp_len[None, :], 0), axis=1)
    owners = jnp.where(
        pack_row >= 0, jnp.sum(jnp.where(hit_table, resp_prompt[None, :], 0), axis=1), -1
    )
    limits = jnp.cumsum(slot_spans)
    row_slot = jnp.sum(
        (jnp.arange(row_count)[:, None] >= limits[None, :]).astype(jnp.int32), axis=1
    )
    return (row_slot, owners)


def prompt_part(p_x, p_bc, p_dt, p_decay, d_skip):
    head_count = p_dt.shape[1]
    groups = lax.axis_size("seq")
    block_heads = head_count // groups
    state_width = p_bc.shape[2] // 2
    inputs, inner_part, gained, local_state, c_rows = block_terms(
        p_x[0], p_bc[0], p_dt[0], p_decay[0], jnp.zeros((STRETCH,), jnp.int32)
    )
    channels = inputs.shape[2]
    block_gain = gained[:, -1]
    pad = 8
    gain_rows = jnp.broadcast_to(block_gain[:, None, None], (head_count, pad, channels))
    payload = jnp.concatenate([local_state, gain_rows], axis=1)
    payload = payload.reshape(groups, block_heads, state_width + pad, channels)
    arrived = lax.all_to_all(payload, "seq", 0, 0, tiled=True)
    pieces = arrived[:, :, :state_width, :]
    log_gains = arrived[:, :, state_width, 0]
    ends = jnp.arange(groups + 1)[:, None, None]
    sources = jnp.arange(groups)[None, :, None]
    between = jnp.arange(groups)[None, None, :]
    spans = (sources < between) & (between < ends)
    exponents = jnp.sum(jnp.where(spans[..., None], log_gains[None, None], 0.0), axis=2)
    weights = jnp.where(sources < ends, jnp.exp(exponents), 0.0)
    states = jnp.sum(weights[:, :, :, None, None] * pieces[None], axis=1)
    own_seed = states[groups].astype(jnp.bfloat16)
    sent_back = states[:groups].astype(jnp.bfloat16)
    prefix = lax.all_to_all(sent_back, "seq", 0, 0, tiled=True)
    prefix = prefix.reshape(head_count, state_width, channels)
    carried = product("in,hnp->ihp", c_rows, prefix) * jnp.exp(gained).T[:, :, None]
    output = inner_part + carried + d_skip[None, :, None] * inputs.astype(jnp.float32)
    p_out = output.reshape(STRETCH, -1).astype(jnp.bfloat16)[None]
    return p_out, own_seed


def response_part(skip_gain, rows_x, rows_bc, rows_dt, rows_decay, row_slot, slot_seeds):
    slot_count = slot_seeds.shape[0]
    blocks = rows_x.shape[0] // STRETCH
    head_count = rows_dt.shape[0]
    state_width = rows_bc.shape[1] // 2
    sliced = (
        rows_x.reshape(blocks, STRETCH, -1),
        rows_bc.reshape(blocks, STRETCH, -1),
        rows_dt.reshape(head_count, blocks, STRETCH).transpose(1, 0, 2),
        rows_decay.reshape(head_count, blocks, STRETCH).transpose(1, 0, 2),
        row_slot.reshape(blocks, STRETCH),
    )
    inputs, inner_part, gained, local_state, c_rows = jax.vmap(block_terms)(*sliced)
    block_slot = sliced[4]
    channels = inputs.shape[3]
    slot_ids = jnp.arange(slot_count)
    seeds_f32 = slot_seeds.astype(jnp.float32)
    block_gain = jnp.exp(gained[:, :, -1])

    state = jnp.zeros((head_count, state_width, channels), jnp.float32)
    previous = jnp.int32(-1)
    continued_bases = []
    continued_flags = []
    for block in range(blocks):
        first_slot = block_slot[block, 0]
        final_slot = block_slot[block, STRETCH - 1]
        carried_on = first_slot == previous
        continued_bases.append(state.astype(jnp.bfloat16))
        continued_flags.append(carried_on)
        fresh_seed = jnp.sum(
            jnp.where((slot_ids == final_slot)[:, None, None, None], seeds_f32, 0.0), axis=0
        )
        anchor = jnp.where((final_slot == first_slot) & carried_on, state, fresh_seed)
        state = block_gain[block][:, None, None] * anchor + local_state[block]
        previous = final_slot
    continued_bases = jnp.stack(continued_bases, axis=0)
    continued_flags = jnp.stack(continued_flags, axis=0)

    hot_rows = (block_slot[:, :, None] == slot_ids[None, None, :]).astype(jnp.bfloat16)
    masked_c = (c_rows[:, :, None, :] * hot_rows[:, :, :, None]).reshape(
        blocks * STRETCH, slot_count * state_width
    )
    seed_table = slot_seeds.transpose(0, 2, 1, 3).reshape(
        slot_count * state_width, head_count * channels
    )
    from_seeds = jnp.dot(masked_c, seed_table, preferred_element_type=jnp.float32)
    from_seeds = from_seeds.reshape(blocks, STRETCH, head_count, channels)
    from_state = product("bin,bhnp->bihp", c_rows, continued_bases)
    continues_row = continued_flags[:, None] & (block_slot == block_slot[:, :1])
    projected = jnp.where(continues_row[:, :, None, None], from_state, from_seeds)
    carried = projected * jnp.exp(gained).transpose(0, 2, 1)[:, :, :, None]
    output = inner_part + carried + skip_gain[None, None, :, None] * inputs.astype(jnp.float32)
    output = jnp.where((block_slot < slot_count)[:, :, None, None], output, 0.0)
    return output.reshape(rows_x.shape).astype(jnp.bfloat16)


def gather_all(piece, axis, radix=4):
    count = lax.axis_size(axis)
    mine = lax.axis_index(axis)
    rounds = 0
    while radix ** rounds < count:
        rounds += 1
    assert radix ** rounds == count
    held = piece
    for level in range(rounds):
        step = radix ** (rounds - 1 - level)
        digit = (mine // step) % radix
        sources = [held]
        for offset in range(1, radix):
            pairs = [(index, index ^ (offset * step)) for index in range(count)]
            sources.append(lax.ppermute(held, axis, pairs))
        sources = jnp.stack(sources, axis=0)
        entries = [
            lax.dynamic_index_in_dim(sources, value ^ digit, 0, keepdims=False)
            for value in range(radix)
        ]
        held = jnp.stack(entries, axis=level)
    return held.reshape((count,) + piece.shape)


def on_device(
    p_x, p_bc, p_dt, p_decay, r_x, r_bc, r_dt, r_decay, pack_list, resp_len, resp_prompt, d_skip
):
    head_count = p_dt.shape[1]
    groups = lax.axis_size("seq")
    block_heads = head_count // groups
    p_out, own_seed = prompt_part(p_x, p_bc, p_dt, p_decay, d_skip)
    own_seed, r_x, r_bc, r_dt, r_decay = lax.optimization_barrier(
        (own_seed, r_x, r_bc, r_dt, r_decay)
    )
    row_slot, owners = slot_layout(pack_list[0], resp_len, resp_prompt, r_x.shape[0])
    gathered_piece = gather_all(own_seed, "grp")
    chosen = (owners[:, None] == jnp.arange(gathered_piece.shape[0])[None, :]).astype(jnp.bfloat16)
    slot_seeds = product("km,mhnp->khnp", chosen, gathered_piece).astype(jnp.bfloat16)
    skip_block = lax.dynamic_slice_in_dim(
        d_skip, lax.axis_index("seq") * block_heads, block_heads, 0
    )
    r_out = response_part(skip_block, r_x, r_bc, r_dt, r_decay, row_slot, slot_seeds)
    return (p_out, r_out)


def solution(mesh):
    placed = (
        P("grp", "seq", None),
        P("grp", "seq", None),
        P("grp", None, "seq"),
        P("grp", None, "seq"),
        P("grp", "seq"),
        P("grp", None),
        P("seq", "grp"),
        P("seq", "grp"),
        P("grp", None),
        P(),
        P(),
        P(),
    )
    return jax.shard_map(
        on_device,
        mesh=mesh,
        in_specs=placed,
        out_specs=(P("grp", "seq", None), P("grp", "seq")),
        check_vma=False,
    )
```

```python
import jax
import jax.numpy as jnp
from jax import lax
from jax.sharding import PartitionSpec as P

STRETCH = 256


def product(einsum_form, left_side, right_side):
    return jnp.einsum(einsum_form, left_side, right_side, preferred_element_type=jnp.float32)


def block_terms(block_x, block_bc, block_dt, block_decay, block_slot):
    length = block_x.shape[0]
    head_count = block_dt.shape[0]
    state_width = block_bc.shape[1] // 2
    inputs = block_x.reshape(length, head_count, -1)
    b_rows = block_bc[:, :state_width]
    c_rows = block_bc[:, state_width:]
    running = jnp.cumsum(block_decay, axis=1)
    before = running - block_decay
    places = jnp.arange(length)
    same_span = (block_slot[:, None] == block_slot[None, :]) & (places[None, :] <= places[:, None])
    starts_here = jnp.concatenate([jnp.ones((1,), jnp.bool_), block_slot[1:] != block_slot[:-1]])
    leader = same_span & starts_here[None, :]
    offset = jnp.sum(jnp.where(leader[None], before[:, None, :], 0.0), axis=2)
    gained = running - offset
    scores = jnp.dot(c_rows, b_rows.T, preferred_element_type=jnp.float32)
    spread = jnp.where(same_span[None], running[:, :, None] - running[:, None, :], -jnp.inf)
    mixing = (jnp.exp(spread) * block_dt[:, None, :] * scores[None]).astype(jnp.bfloat16)
    inner_part = product("hij,jhp->ihp", mixing, inputs)
    tail_rows = block_slot == block_slot[length - 1]
    to_end = jnp.where(tail_rows[None], jnp.exp(running[:, length - 1 :] - running) * block_dt, 0.0)
    scaled = (to_end[:, :, None] * b_rows[None].astype(jnp.float32)).astype(jnp.bfloat16)
    local_state = product("hjn,jhp->hnp", scaled, inputs)
    return (inputs, inner_part, gained, local_state, c_rows)


def slot_layout(pack_row, resp_len, resp_prompt, row_count):
    hit_table = pack_row[:, None] == jnp.arange(resp_len.shape[0])[None, :]
    slot_spans = jnp.sum(jnp.where(hit_table, resp_len[None, :], 0), axis=1)
    owners = jnp.where(
        pack_row >= 0, jnp.sum(jnp.where(hit_table, resp_prompt[None, :], 0), axis=1), -1
    )
    limits = jnp.cumsum(slot_spans)
    row_slot = jnp.sum(
        (jnp.arange(row_count)[:, None] >= limits[None, :]).astype(jnp.int32), axis=1
    )
    return (row_slot, owners)


def prompt_part(p_x, p_bc, p_dt, p_decay, d_skip):
    head_count = p_dt.shape[1]
    groups = lax.axis_size("seq")
    block_heads = head_count // groups
    state_width = p_bc.shape[2] // 2
    inputs, inner_part, gained, local_state, c_rows = block_terms(
        p_x[0], p_bc[0], p_dt[0], p_decay[0], jnp.zeros((STRETCH,), jnp.int32)
    )
    channels = inputs.shape[2]
    block_gain = gained[:, -1]
    pad = 8
    gain_rows = jnp.broadcast_to(block_gain[:, None, None], (head_count, pad, channels))
    payload = jnp.concatenate([local_state, gain_rows], axis=1)
    payload = payload.reshape(groups, block_heads, state_width + pad, channels)
    arrived = lax.all_to_all(payload, "seq", 0, 0, tiled=True)
    pieces = arrived[:, :, :state_width, :]
    log_gains = arrived[:, :, state_width, 0]
    ends = jnp.arange(groups + 1)[:, None, None]
    sources = jnp.arange(groups)[None, :, None]
    between = jnp.arange(groups)[None, None, :]
    spans = (sources < between) & (between < ends)
    exponents = jnp.sum(jnp.where(spans[..., None], log_gains[None, None], 0.0), axis=2)
    weights = jnp.where(sources < ends, jnp.exp(exponents), 0.0)
    states = jnp.sum(weights[:, :, :, None, None] * pieces[None], axis=1)
    own_seed = states[groups].astype(jnp.bfloat16)
    sent_back = states[:groups].astype(jnp.bfloat16)
    prefix = lax.all_to_all(sent_back, "seq", 0, 0, tiled=True)
    prefix = prefix.reshape(head_count, state_width, channels)
    carried = product("in,hnp->ihp", c_rows, prefix) * jnp.exp(gained).T[:, :, None]
    output = inner_part + carried + d_skip[None, :, None] * inputs.astype(jnp.float32)
    p_out = output.reshape(STRETCH, -1).astype(jnp.bfloat16)[None]
    return p_out, own_seed


def response_part(skip_gain, rows_x, rows_bc, rows_dt, rows_decay, row_slot, slot_seeds):
    slot_count = slot_seeds.shape[0]
    blocks = rows_x.shape[0] // STRETCH
    head_count = rows_dt.shape[0]
    state_width = rows_bc.shape[1] // 2
    sliced = (
        rows_x.reshape(blocks, STRETCH, -1),
        rows_bc.reshape(blocks, STRETCH, -1),
        rows_dt.reshape(head_count, blocks, STRETCH).transpose(1, 0, 2),
        rows_decay.reshape(head_count, blocks, STRETCH).transpose(1, 0, 2),
        row_slot.reshape(blocks, STRETCH),
    )
    inputs, inner_part, gained, local_state, c_rows = jax.vmap(block_terms)(*sliced)
    block_slot = sliced[4]
    channels = inputs.shape[3]
    slot_ids = jnp.arange(slot_count)
    seeds_f32 = slot_seeds.astype(jnp.float32)
    block_gain = jnp.exp(gained[:, :, -1])

    state = jnp.zeros((head_count, state_width, channels), jnp.float32)
    previous = jnp.int32(-1)
    continued_bases = []
    continued_flags = []
    for block in range(blocks):
        first_slot = block_slot[block, 0]
        final_slot = block_slot[block, STRETCH - 1]
        carried_on = first_slot == previous
        continued_bases.append(state.astype(jnp.bfloat16))
        continued_flags.append(carried_on)
        fresh_seed = jnp.sum(
            jnp.where((slot_ids == final_slot)[:, None, None, None], seeds_f32, 0.0), axis=0
        )
        anchor = jnp.where((final_slot == first_slot) & carried_on, state, fresh_seed)
        state = block_gain[block][:, None, None] * anchor + local_state[block]
        previous = final_slot
    continued_bases = jnp.stack(continued_bases, axis=0)
    continued_flags = jnp.stack(continued_flags, axis=0)

    hot_rows = (block_slot[:, :, None] == slot_ids[None, None, :]).astype(jnp.bfloat16)
    masked_c = (c_rows[:, :, None, :] * hot_rows[:, :, :, None]).reshape(
        blocks * STRETCH, slot_count * state_width
    )
    seed_table = slot_seeds.transpose(0, 2, 1, 3).reshape(
        slot_count * state_width, head_count * channels
    )
    from_seeds = jnp.dot(masked_c, seed_table, preferred_element_type=jnp.float32)
    from_seeds = from_seeds.reshape(blocks, STRETCH, head_count, channels)
    from_state = product("bin,bhnp->bihp", c_rows, continued_bases)
    continues_row = continued_flags[:, None] & (block_slot == block_slot[:, :1])
    projected = jnp.where(continues_row[:, :, None, None], from_state, from_seeds)
    carried = projected * jnp.exp(gained).transpose(0, 2, 1)[:, :, :, None]
    output = inner_part + carried + skip_gain[None, None, :, None] * inputs.astype(jnp.float32)
    output = jnp.where((block_slot < slot_count)[:, :, None, None], output, 0.0)
    return output.reshape(rows_x.shape).astype(jnp.bfloat16)


def gather_all(piece, axis, radix=4):
    count = lax.axis_size(axis)
    mine = lax.axis_index(axis)
    rounds = 0
    while radix ** rounds < count:
        rounds += 1
    assert radix ** rounds == count
    held = piece
    for level in range(rounds):
        step = radix ** (rounds - 1 - level)
        digit = (mine // step) % radix
        sources = [held]
        for offset in range(1, radix):
            pairs = [(index, index ^ (offset * step)) for index in range(count)]
            sources.append(lax.ppermute(held, axis, pairs))
        sources = jnp.stack(sources, axis=0)
        entries = [
            lax.dynamic_index_in_dim(sources, value ^ digit, 0, keepdims=False)
            for value in range(radix)
        ]
        held = jnp.stack(entries, axis=level)
    return held.reshape((count,) + piece.shape)


def on_device(
    p_x, p_bc, p_dt, p_decay, r_x, r_bc, r_dt, r_decay, pack_list, resp_len, resp_prompt, d_skip
):
    head_count = p_dt.shape[1]
    groups = lax.axis_size("seq")
    block_heads = head_count // groups
    p_out, own_seed = prompt_part(p_x, p_bc, p_dt, p_decay, d_skip)
    own_seed, r_x, r_bc, r_dt, r_decay = lax.optimization_barrier(
        (own_seed, r_x, r_bc, r_dt, r_decay)
    )
    row_slot, owners = slot_layout(pack_list[0], resp_len, resp_prompt, r_x.shape[0])
    sibling = lax.ppermute(own_seed, "core", [(0, 1), (1, 0)])
    first_core = lax.axis_index("core") == 0
    pair = jnp.stack(
        [jnp.where(first_core, own_seed, sibling), jnp.where(first_core, sibling, own_seed)]
    )
    gathered_piece = lax.all_gather(pair, "zz", axis=0, tiled=True)
    chosen = (owners[:, None] == jnp.arange(gathered_piece.shape[0])[None, :]).astype(jnp.bfloat16)
    slot_seeds = product("km,mhnp->khnp", chosen, gathered_piece).astype(jnp.bfloat16)
    skip_block = lax.dynamic_slice_in_dim(
        d_skip, lax.axis_index("seq") * block_heads, block_heads, 0
    )
    r_out = response_part(skip_block, r_x, r_bc, r_dt, r_decay, row_slot, slot_seeds)
    return (p_out, r_out)


def solution(mesh):
    devices = mesh.devices
    split = jax.sharding.Mesh(
        devices.reshape(devices.shape[0], devices.shape[1] // 2, 2), ("seq", "zz", "core")
    )
    grp = ("zz", "core")
    placed = (
        P(grp, "seq", None),
        P(grp, "seq", None),
        P(grp, None, "seq"),
        P(grp, None, "seq"),
        P(grp, "seq"),
        P(grp, None),
        P("seq", grp),
        P("seq", grp),
        P(grp, None),
        P(),
        P(),
        P(),
    )
    return jax.shard_map(
        on_device,
        mesh=split,
        in_specs=placed,
        out_specs=(P(grp, "seq", None), P(grp, "seq")),
        check_vma=False,
    )
```

```python
import jax
import jax.numpy as jnp
from jax import lax
from jax.sharding import PartitionSpec as P

STRETCH = 256


def product(einsum_form, left_side, right_side):
    return jnp.einsum(einsum_form, left_side, right_side, preferred_element_type=jnp.float32)


def block_terms(block_x, block_bc, block_dt, block_decay, block_slot):
    length = block_x.shape[0]
    head_count = block_dt.shape[0]
    state_width = block_bc.shape[1] // 2
    inputs = block_x.reshape(length, head_count, -1)
    b_rows = block_bc[:, :state_width]
    c_rows = block_bc[:, state_width:]
    running = jnp.cumsum(block_decay, axis=1)
    before = running - block_decay
    places = jnp.arange(length)
    same_span = (block_slot[:, None] == block_slot[None, :]) & (places[None, :] <= places[:, None])
    starts_here = jnp.concatenate([jnp.ones((1,), jnp.bool_), block_slot[1:] != block_slot[:-1]])
    leader = same_span & starts_here[None, :]
    offset = jnp.sum(jnp.where(leader[None], before[:, None, :], 0.0), axis=2)
    gained = running - offset
    scores = jnp.dot(c_rows, b_rows.T, preferred_element_type=jnp.float32)
    spread = jnp.where(same_span[None], running[:, :, None] - running[:, None, :], -jnp.inf)
    mixing = (jnp.exp(spread) * block_dt[:, None, :] * scores[None]).astype(jnp.bfloat16)
    inner_part = product("hij,jhp->ihp", mixing, inputs)
    tail_rows = block_slot == block_slot[length - 1]
    to_end = jnp.where(tail_rows[None], jnp.exp(running[:, length - 1 :] - running) * block_dt, 0.0)
    scaled = (to_end[:, :, None] * b_rows[None].astype(jnp.float32)).astype(jnp.bfloat16)
    local_state = product("hjn,jhp->hnp", scaled, inputs)
    return (inputs, inner_part, gained, local_state, c_rows)


def slot_layout(pack_row, resp_len, resp_prompt, row_count):
    hit_table = pack_row[:, None] == jnp.arange(resp_len.shape[0])[None, :]
    slot_spans = jnp.sum(jnp.where(hit_table, resp_len[None, :], 0), axis=1)
    owners = jnp.where(
        pack_row >= 0, jnp.sum(jnp.where(hit_table, resp_prompt[None, :], 0), axis=1), -1
    )
    limits = jnp.cumsum(slot_spans)
    row_slot = jnp.sum(
        (jnp.arange(row_count)[:, None] >= limits[None, :]).astype(jnp.int32), axis=1
    )
    return (row_slot, owners)


def prompt_part(p_x, p_bc, p_dt, p_decay, d_skip):
    head_count = p_dt.shape[1]
    groups = lax.axis_size("seq")
    block_heads = head_count // groups
    state_width = p_bc.shape[2] // 2
    inputs, inner_part, gained, local_state, c_rows = block_terms(
        p_x[0], p_bc[0], p_dt[0], p_decay[0], jnp.zeros((STRETCH,), jnp.int32)
    )
    channels = inputs.shape[2]
    block_gain = gained[:, -1]
    pad = 8
    gain_rows = jnp.broadcast_to(block_gain[:, None, None], (head_count, pad, channels))
    payload = jnp.concatenate([local_state, gain_rows], axis=1)
    payload = payload.reshape(groups, block_heads, state_width + pad, channels)
    arrived = lax.all_to_all(payload, "seq", 0, 0, tiled=True)
    pieces = arrived[:, :, :state_width, :]
    log_gains = arrived[:, :, state_width, 0]
    ends = jnp.arange(groups + 1)[:, None, None]
    sources = jnp.arange(groups)[None, :, None]
    between = jnp.arange(groups)[None, None, :]
    spans = (sources < between) & (between < ends)
    exponents = jnp.sum(jnp.where(spans[..., None], log_gains[None, None], 0.0), axis=2)
    weights = jnp.where(sources < ends, jnp.exp(exponents), 0.0)
    states = jnp.sum(weights[:, :, :, None, None] * pieces[None], axis=1)
    own_seed = states[groups].astype(jnp.bfloat16)
    sent_back = states[:groups].astype(jnp.bfloat16)
    prefix = lax.all_to_all(sent_back, "seq", 0, 0, tiled=True)
    prefix = prefix.reshape(head_count, state_width, channels)
    carried = product("in,hnp->ihp", c_rows, prefix) * jnp.exp(gained).T[:, :, None]
    output = inner_part + carried + d_skip[None, :, None] * inputs.astype(jnp.float32)
    p_out = output.reshape(STRETCH, -1).astype(jnp.bfloat16)[None]
    return p_out, own_seed


def response_part(skip_gain, rows_x, rows_bc, rows_dt, rows_decay, row_slot, slot_seeds):
    slot_count = slot_seeds.shape[0]
    blocks = rows_x.shape[0] // STRETCH
    head_count = rows_dt.shape[0]
    state_width = rows_bc.shape[1] // 2
    sliced = (
        rows_x.reshape(blocks, STRETCH, -1),
        rows_bc.reshape(blocks, STRETCH, -1),
        rows_dt.reshape(head_count, blocks, STRETCH).transpose(1, 0, 2),
        rows_decay.reshape(head_count, blocks, STRETCH).transpose(1, 0, 2),
        row_slot.reshape(blocks, STRETCH),
    )
    inputs, inner_part, gained, local_state, c_rows = jax.vmap(block_terms)(*sliced)
    block_slot = sliced[4]
    channels = inputs.shape[3]
    slot_ids = jnp.arange(slot_count)
    seeds_f32 = slot_seeds.astype(jnp.float32)
    block_gain = jnp.exp(gained[:, :, -1])

    state = jnp.zeros((head_count, state_width, channels), jnp.float32)
    previous = jnp.int32(-1)
    continued_bases = []
    continued_flags = []
    for block in range(blocks):
        first_slot = block_slot[block, 0]
        final_slot = block_slot[block, STRETCH - 1]
        carried_on = first_slot == previous
        continued_bases.append(state.astype(jnp.bfloat16))
        continued_flags.append(carried_on)
        fresh_seed = jnp.sum(
            jnp.where((slot_ids == final_slot)[:, None, None, None], seeds_f32, 0.0), axis=0
        )
        anchor = jnp.where((final_slot == first_slot) & carried_on, state, fresh_seed)
        state = block_gain[block][:, None, None] * anchor + local_state[block]
        previous = final_slot
    continued_bases = jnp.stack(continued_bases, axis=0)
    continued_flags = jnp.stack(continued_flags, axis=0)

    hot_rows = (block_slot[:, :, None] == slot_ids[None, None, :]).astype(jnp.float32)
    seed_table = slot_seeds.transpose(2, 0, 1, 3).reshape(
        state_width, slot_count * head_count * channels
    )
    every_slot = jnp.dot(
        c_rows.reshape(blocks * STRETCH, state_width), seed_table, preferred_element_type=jnp.float32
    )
    every_slot = every_slot.reshape(blocks, STRETCH, slot_count, head_count, channels)
    from_seeds = jnp.sum(every_slot * hot_rows[:, :, :, None, None], axis=2)
    from_state = product("bin,bhnp->bihp", c_rows, continued_bases)
    continues_row = continued_flags[:, None] & (block_slot == block_slot[:, :1])
    projected = jnp.where(continues_row[:, :, None, None], from_state, from_seeds)
    carried = projected * jnp.exp(gained).transpose(0, 2, 1)[:, :, :, None]
    output = inner_part + carried + skip_gain[None, None, :, None] * inputs.astype(jnp.float32)
    output = jnp.where((block_slot < slot_count)[:, :, None, None], output, 0.0)
    return output.reshape(rows_x.shape).astype(jnp.bfloat16)


def gather_all(piece, axis, radix=4):
    count = lax.axis_size(axis)
    mine = lax.axis_index(axis)
    rounds = 0
    while radix ** rounds < count:
        rounds += 1
    assert radix ** rounds == count
    held = piece
    for level in range(rounds):
        step = radix ** (rounds - 1 - level)
        digit = (mine // step) % radix
        sources = [held]
        for offset in range(1, radix):
            pairs = [(index, index ^ (offset * step)) for index in range(count)]
            sources.append(lax.ppermute(held, axis, pairs))
        sources = jnp.stack(sources, axis=0)
        entries = [
            lax.dynamic_index_in_dim(sources, value ^ digit, 0, keepdims=False)
            for value in range(radix)
        ]
        held = jnp.stack(entries, axis=level)
    return held.reshape((count,) + piece.shape)


def on_device(
    p_x, p_bc, p_dt, p_decay, r_x, r_bc, r_dt, r_decay, pack_list, resp_len, resp_prompt, d_skip
):
    head_count = p_dt.shape[1]
    groups = lax.axis_size("seq")
    block_heads = head_count // groups
    p_out, own_seed = prompt_part(p_x, p_bc, p_dt, p_decay, d_skip)
    own_seed, r_x, r_bc, r_dt, r_decay = lax.optimization_barrier(
        (own_seed, r_x, r_bc, r_dt, r_decay)
    )
    row_slot, owners = slot_layout(pack_list[0], resp_len, resp_prompt, r_x.shape[0])
    gathered_piece = gather_all(own_seed, "grp")
    chosen = (owners[:, None] == jnp.arange(gathered_piece.shape[0])[None, :]).astype(jnp.bfloat16)
    slot_seeds = product("km,mhnp->khnp", chosen, gathered_piece).astype(jnp.bfloat16)
    skip_block = lax.dynamic_slice_in_dim(
        d_skip, lax.axis_index("seq") * block_heads, block_heads, 0
    )
    r_out = response_part(skip_block, r_x, r_bc, r_dt, r_decay, row_slot, slot_seeds)
    return (p_out, r_out)


def solution(mesh):
    placed = (
        P("grp", "seq", None),
        P("grp", "seq", None),
        P("grp", None, "seq"),
        P("grp", None, "seq"),
        P("grp", "seq"),
        P("grp", None),
        P("seq", "grp"),
        P("seq", "grp"),
        P("grp", None),
        P(),
        P(),
        P(),
    )
    return jax.shard_map(
        on_device,
        mesh=mesh,
        in_specs=placed,
        out_specs=(P("grp", "seq", None), P("grp", "seq")),
        check_vma=False,
    )
```

```python
import math

import jax
import jax.numpy as jnp
from jax import lax
from jax.sharding import PartitionSpec as P

STRETCH = 256


def product(einsum_form, left_side, right_side):
    return jnp.einsum(einsum_form, left_side, right_side, preferred_element_type=jnp.float32)


def block_terms(block_x, block_bc, block_dt, block_decay, block_slot):
    length = block_x.shape[0]
    head_count = block_dt.shape[0]
    state_width = block_bc.shape[1] // 2
    inputs = block_x.reshape(length, head_count, -1)
    b_rows = block_bc[:, :state_width]
    c_rows = block_bc[:, state_width:]
    running = jnp.cumsum(block_decay, axis=1)
    before = running - block_decay
    places = jnp.arange(length)
    same_span = (block_slot[:, None] == block_slot[None, :]) & (places[None, :] <= places[:, None])
    starts_here = jnp.concatenate([jnp.ones((1,), jnp.bool_), block_slot[1:] != block_slot[:-1]])
    leader = same_span & starts_here[None, :]
    offset = jnp.sum(jnp.where(leader[None], before[:, None, :], 0.0), axis=2)
    gained = running - offset
    scores = jnp.dot(c_rows, b_rows.T, preferred_element_type=jnp.float32)
    spread = jnp.where(same_span[None], running[:, :, None] - running[:, None, :], -jnp.inf)
    mixing = (jnp.exp(spread) * block_dt[:, None, :] * scores[None]).astype(jnp.bfloat16)
    inner_part = product("hij,jhp->ihp", mixing, inputs)
    tail_rows = block_slot == block_slot[length - 1]
    to_end = jnp.where(tail_rows[None], jnp.exp(running[:, length - 1 :] - running) * block_dt, 0.0)
    scaled = (to_end[:, :, None] * b_rows[None].astype(jnp.float32)).astype(jnp.bfloat16)
    local_state = product("hjn,jhp->hnp", scaled, inputs)
    return (inputs, inner_part, gained, local_state, c_rows)


def slot_layout(pack_row, resp_len, resp_prompt, row_count):
    hit_table = pack_row[:, None] == jnp.arange(resp_len.shape[0])[None, :]
    slot_spans = jnp.sum(jnp.where(hit_table, resp_len[None, :], 0), axis=1)
    owners = jnp.where(
        pack_row >= 0, jnp.sum(jnp.where(hit_table, resp_prompt[None, :], 0), axis=1), -1
    )
    limits = jnp.cumsum(slot_spans)
    row_slot = jnp.sum(
        (jnp.arange(row_count)[:, None] >= limits[None, :]).astype(jnp.int32), axis=1
    )
    return (row_slot, owners)


def prompt_part(p_x, p_bc, p_dt, p_decay, d_skip):
    head_count = p_dt.shape[1]
    groups = lax.axis_size("seq")
    block_heads = head_count // groups
    state_width = p_bc.shape[2] // 2
    inputs, inner_part, gained, local_state, c_rows = block_terms(
        p_x[0], p_bc[0], p_dt[0], p_decay[0], jnp.zeros((STRETCH,), jnp.int32)
    )
    channels = inputs.shape[2]
    block_gain = gained[:, -1]
    pad = 8
    gain_rows = jnp.broadcast_to(block_gain[:, None, None], (head_count, pad, channels))
    payload = jnp.concatenate([local_state, gain_rows], axis=1)
    payload = payload.reshape(groups, block_heads, state_width + pad, channels)
    arrived = lax.all_to_all(payload, "seq", 0, 0, tiled=True)
    pieces = arrived[:, :, :state_width, :]
    log_gains = arrived[:, :, state_width, 0]
    ends = jnp.arange(groups + 1)[:, None, None]
    sources = jnp.arange(groups)[None, :, None]
    between = jnp.arange(groups)[None, None, :]
    spans = (sources < between) & (between < ends)
    exponents = jnp.sum(jnp.where(spans[..., None], log_gains[None, None], 0.0), axis=2)
    weights = jnp.where(sources < ends, jnp.exp(exponents), 0.0)
    states = jnp.sum(weights[:, :, :, None, None] * pieces[None], axis=1)
    own_seed = states[groups].astype(jnp.bfloat16)
    sent_back = states[:groups].astype(jnp.bfloat16)
    prefix = lax.all_to_all(sent_back, "seq", 0, 0, tiled=True)
    prefix = prefix.reshape(head_count, state_width, channels)
    carried = product("in,hnp->ihp", c_rows, prefix) * jnp.exp(gained).T[:, :, None]
    output = inner_part + carried + d_skip[None, :, None] * inputs.astype(jnp.float32)
    p_out = output.reshape(STRETCH, -1).astype(jnp.bfloat16)[None]
    return p_out, own_seed


def response_part(skip_gain, rows_x, rows_bc, rows_dt, rows_decay, row_slot, slot_seeds):
    slot_count = slot_seeds.shape[0]
    blocks = rows_x.shape[0] // STRETCH
    head_count = rows_dt.shape[0]
    state_width = rows_bc.shape[1] // 2
    sliced = (
        rows_x.reshape(blocks, STRETCH, -1),
        rows_bc.reshape(blocks, STRETCH, -1),
        rows_dt.reshape(head_count, blocks, STRETCH).transpose(1, 0, 2),
        rows_decay.reshape(head_count, blocks, STRETCH).transpose(1, 0, 2),
        row_slot.reshape(blocks, STRETCH),
    )
    inputs, inner_part, gained, local_state, c_rows = jax.vmap(block_terms)(*sliced)
    block_slot = sliced[4]
    channels = inputs.shape[3]
    slot_ids = jnp.arange(slot_count)
    seeds_f32 = slot_seeds.astype(jnp.float32)
    block_gain = jnp.exp(gained[:, :, -1])

    state = jnp.zeros((head_count, state_width, channels), jnp.float32)
    previous = jnp.int32(-1)
    continued_bases = []
    continued_flags = []
    for block in range(blocks):
        first_slot = block_slot[block, 0]
        final_slot = block_slot[block, STRETCH - 1]
        carried_on = first_slot == previous
        continued_bases.append(state.astype(jnp.bfloat16))
        continued_flags.append(carried_on)
        fresh_seed = jnp.sum(
            jnp.where((slot_ids == final_slot)[:, None, None, None], seeds_f32, 0.0), axis=0
        )
        anchor = jnp.where((final_slot == first_slot) & carried_on, state, fresh_seed)
        state = block_gain[block][:, None, None] * anchor + local_state[block]
        previous = final_slot
    continued_bases = jnp.stack(continued_bases, axis=0)
    continued_flags = jnp.stack(continued_flags, axis=0)

    hot_rows = (block_slot[:, :, None] == slot_ids[None, None, :]).astype(jnp.float32)
    seed_table = slot_seeds.transpose(2, 0, 1, 3).reshape(
        state_width, slot_count * head_count * channels
    )
    every_slot = jnp.dot(
        c_rows.reshape(blocks * STRETCH, state_width), seed_table, preferred_element_type=jnp.float32
    )
    every_slot = every_slot.reshape(blocks, STRETCH, slot_count, head_count, channels)
    from_seeds = jnp.sum(every_slot * hot_rows[:, :, :, None, None], axis=2)
    from_state = product("bin,bhnp->bihp", c_rows, continued_bases)
    continues_row = continued_flags[:, None] & (block_slot == block_slot[:, :1])
    projected = jnp.where(continues_row[:, :, None, None], from_state, from_seeds)
    carried = projected * jnp.exp(gained).transpose(0, 2, 1)[:, :, :, None]
    output = inner_part + carried + skip_gain[None, None, :, None] * inputs.astype(jnp.float32)
    output = jnp.where((block_slot < slot_count)[:, :, None, None], output, 0.0)
    return output.reshape(rows_x.shape).astype(jnp.bfloat16)


def gather_all(piece, axis, radices):
    count = lax.axis_size(axis)
    mine = lax.axis_index(axis)
    assert math.prod(radices) == count
    held = piece
    for level, radix in enumerate(radices):
        step = math.prod(radices[level + 1 :])
        digit = (mine // step) % radix
        sources = [held]
        for offset in range(1, radix):
            pairs = [(index, index ^ (offset * step)) for index in range(count)]
            sources.append(lax.ppermute(held, axis, pairs))
        sources = jnp.stack(sources, axis=0)
        entries = [
            lax.dynamic_index_in_dim(sources, value ^ digit, 0, keepdims=False)
            for value in range(radix)
        ]
        held = jnp.stack(entries, axis=level)
    return held.reshape((count,) + piece.shape)


def on_device(
    p_x, p_bc, p_dt, p_decay, r_x, r_bc, r_dt, r_decay, pack_list, resp_len, resp_prompt, d_skip
):
    head_count = p_dt.shape[1]
    groups = lax.axis_size("seq")
    block_heads = head_count // groups
    p_out, own_seed = prompt_part(p_x, p_bc, p_dt, p_decay, d_skip)
    own_seed, r_x, r_bc, r_dt, r_decay = lax.optimization_barrier(
        (own_seed, r_x, r_bc, r_dt, r_decay)
    )
    row_slot, owners = slot_layout(pack_list[0], resp_len, resp_prompt, r_x.shape[0])
    gathered_piece = gather_all(own_seed, "grp", (4, 4, 2, 2))
    chosen = (owners[:, None] == jnp.arange(gathered_piece.shape[0])[None, :]).astype(jnp.bfloat16)
    slot_seeds = product("km,mhnp->khnp", chosen, gathered_piece).astype(jnp.bfloat16)
    skip_block = lax.dynamic_slice_in_dim(
        d_skip, lax.axis_index("seq") * block_heads, block_heads, 0
    )
    r_out = response_part(skip_block, r_x, r_bc, r_dt, r_decay, row_slot, slot_seeds)
    return (p_out, r_out)


def solution(mesh):
    placed = (
        P("grp", "seq", None),
        P("grp", "seq", None),
        P("grp", None, "seq"),
        P("grp", None, "seq"),
        P("grp", "seq"),
        P("grp", None),
        P("seq", "grp"),
        P("seq", "grp"),
        P("grp", None),
        P(),
        P(),
        P(),
    )
    return jax.shard_map(
        on_device,
        mesh=mesh,
        in_specs=placed,
        out_specs=(P("grp", "seq", None), P("grp", "seq")),
        check_vma=False,
    )
```

```python
import math

import jax
import jax.numpy as jnp
from jax import lax
from jax.sharding import PartitionSpec as P

STRETCH = 256


def product(einsum_form, left_side, right_side):
    return jnp.einsum(einsum_form, left_side, right_side, preferred_element_type=jnp.float32)


def block_terms(block_x, block_bc, block_dt, block_decay, block_slot):
    length = block_x.shape[0]
    head_count = block_dt.shape[0]
    state_width = block_bc.shape[1] // 2
    inputs = block_x.reshape(length, head_count, -1)
    b_rows = block_bc[:, :state_width]
    c_rows = block_bc[:, state_width:]
    running = jnp.cumsum(block_decay, axis=1)
    before = running - block_decay
    places = jnp.arange(length)
    same_span = (block_slot[:, None] == block_slot[None, :]) & (places[None, :] <= places[:, None])
    starts_here = jnp.concatenate([jnp.ones((1,), jnp.bool_), block_slot[1:] != block_slot[:-1]])
    leader = same_span & starts_here[None, :]
    offset = jnp.sum(jnp.where(leader[None], before[:, None, :], 0.0), axis=2)
    gained = running - offset
    scores = jnp.dot(c_rows, b_rows.T, preferred_element_type=jnp.float32)
    spread = jnp.where(same_span[None], running[:, :, None] - running[:, None, :], -jnp.inf)
    mixing = (jnp.exp(spread) * block_dt[:, None, :] * scores[None]).astype(jnp.bfloat16)
    inner_part = product("hij,jhp->ihp", mixing, inputs)
    tail_rows = block_slot == block_slot[length - 1]
    to_end = jnp.where(tail_rows[None], jnp.exp(running[:, length - 1 :] - running) * block_dt, 0.0)
    scaled = (to_end[:, :, None] * b_rows[None].astype(jnp.float32)).astype(jnp.bfloat16)
    local_state = product("hjn,jhp->hnp", scaled, inputs)
    return (inputs, inner_part, gained, local_state, c_rows)


def slot_layout(pack_row, resp_len, resp_prompt, row_count):
    hit_table = pack_row[:, None] == jnp.arange(resp_len.shape[0])[None, :]
    slot_spans = jnp.sum(jnp.where(hit_table, resp_len[None, :], 0), axis=1)
    owners = jnp.where(
        pack_row >= 0, jnp.sum(jnp.where(hit_table, resp_prompt[None, :], 0), axis=1), -1
    )
    limits = jnp.cumsum(slot_spans)
    row_slot = jnp.sum(
        (jnp.arange(row_count)[:, None] >= limits[None, :]).astype(jnp.int32), axis=1
    )
    return (row_slot, owners)


def prompt_part(p_x, p_bc, p_dt, p_decay, d_skip):
    head_count = p_dt.shape[1]
    groups = lax.axis_size("seq")
    block_heads = head_count // groups
    state_width = p_bc.shape[2] // 2
    inputs, inner_part, gained, local_state, c_rows = block_terms(
        p_x[0], p_bc[0], p_dt[0], p_decay[0], jnp.zeros((STRETCH,), jnp.int32)
    )
    channels = inputs.shape[2]
    block_gain = gained[:, -1]
    pad = 8
    gain_rows = jnp.broadcast_to(block_gain[:, None, None], (head_count, pad, channels))
    payload = jnp.concatenate([local_state, gain_rows], axis=1)
    payload = payload.reshape(groups, block_heads, state_width + pad, channels)
    arrived = lax.all_to_all(payload, "seq", 0, 0, tiled=True)
    pieces = arrived[:, :, :state_width, :]
    log_gains = arrived[:, :, state_width, 0]
    ends = jnp.arange(groups + 1)[:, None, None]
    sources = jnp.arange(groups)[None, :, None]
    between = jnp.arange(groups)[None, None, :]
    spans = (sources < between) & (between < ends)
    exponents = jnp.sum(jnp.where(spans[..., None], log_gains[None, None], 0.0), axis=2)
    weights = jnp.where(sources < ends, jnp.exp(exponents), 0.0)
    states = jnp.sum(weights[:, :, :, None, None] * pieces[None], axis=1)
    own_seed = states[groups].astype(jnp.bfloat16)
    sent_back = states[:groups].astype(jnp.bfloat16)
    prefix = lax.all_to_all(sent_back, "seq", 0, 0, tiled=True)
    prefix = prefix.reshape(head_count, state_width, channels)
    carried = product("in,hnp->ihp", c_rows, prefix) * jnp.exp(gained).T[:, :, None]
    output = inner_part + carried + d_skip[None, :, None] * inputs.astype(jnp.float32)
    p_out = output.reshape(STRETCH, -1).astype(jnp.bfloat16)[None]
    return p_out, own_seed


def response_part(skip_gain, rows_x, rows_bc, rows_dt, rows_decay, row_slot, slot_seeds):
    slot_count = slot_seeds.shape[0]
    blocks = rows_x.shape[0] // STRETCH
    head_count = rows_dt.shape[0]
    state_width = rows_bc.shape[1] // 2
    sliced = (
        rows_x.reshape(blocks, STRETCH, -1),
        rows_bc.reshape(blocks, STRETCH, -1),
        rows_dt.reshape(head_count, blocks, STRETCH).transpose(1, 0, 2),
        rows_decay.reshape(head_count, blocks, STRETCH).transpose(1, 0, 2),
        row_slot.reshape(blocks, STRETCH),
    )
    inputs, inner_part, gained, local_state, c_rows = jax.vmap(block_terms)(*sliced)
    block_slot = sliced[4]
    channels = inputs.shape[3]
    slot_ids = jnp.arange(slot_count)
    seeds_f32 = slot_seeds.astype(jnp.float32)
    block_gain = jnp.exp(gained[:, :, -1])

    state = jnp.zeros((head_count, state_width, channels), jnp.float32)
    previous = jnp.int32(-1)
    continued_bases = []
    continued_flags = []
    for block in range(blocks):
        first_slot = block_slot[block, 0]
        final_slot = block_slot[block, STRETCH - 1]
        carried_on = first_slot == previous
        continued_bases.append(state.astype(jnp.bfloat16))
        continued_flags.append(carried_on)
        fresh_seed = jnp.sum(
            jnp.where((slot_ids == final_slot)[:, None, None, None], seeds_f32, 0.0), axis=0
        )
        anchor = jnp.where((final_slot == first_slot) & carried_on, state, fresh_seed)
        state = block_gain[block][:, None, None] * anchor + local_state[block]
        previous = final_slot
    continued_bases = jnp.stack(continued_bases, axis=0)
    continued_flags = jnp.stack(continued_flags, axis=0)

    hot_rows = (block_slot[:, :, None] == slot_ids[None, None, :]).astype(jnp.float32)
    seed_table = slot_seeds.transpose(2, 0, 1, 3).reshape(
        state_width, slot_count * head_count * channels
    )
    every_slot = jnp.dot(
        c_rows.reshape(blocks * STRETCH, state_width), seed_table, preferred_element_type=jnp.float32
    )
    every_slot = every_slot.reshape(blocks, STRETCH, slot_count, head_count, channels)
    from_seeds = jnp.sum(every_slot * hot_rows[:, :, :, None, None], axis=2)
    from_state = product("bin,bhnp->bihp", c_rows, continued_bases)
    continues_row = continued_flags[:, None] & (block_slot == block_slot[:, :1])
    projected = jnp.where(continues_row[:, :, None, None], from_state, from_seeds)
    carried = projected * jnp.exp(gained).transpose(0, 2, 1)[:, :, :, None]
    output = inner_part + carried + skip_gain[None, None, :, None] * inputs.astype(jnp.float32)
    output = jnp.where((block_slot < slot_count)[:, :, None, None], output, 0.0)
    return output.reshape(rows_x.shape).astype(jnp.bfloat16)


def gather_all(piece, axis, radices):
    count = lax.axis_size(axis)
    mine = lax.axis_index(axis)
    assert math.prod(radices) == count
    held = piece
    for level, radix in enumerate(radices):
        step = math.prod(radices[level + 1 :])
        digit = (mine // step) % radix
        sources = [held]
        for offset in range(1, radix):
            pairs = [(index, index ^ (offset * step)) for index in range(count)]
            sources.append(lax.ppermute(held, axis, pairs))
        sources = jnp.stack(sources, axis=0)
        entries = [
            lax.dynamic_index_in_dim(sources, value ^ digit, 0, keepdims=False)
            for value in range(radix)
        ]
        held = jnp.stack(entries, axis=level)
    return held.reshape((count,) + piece.shape)


def on_device(
    p_x, p_bc, p_dt, p_decay, r_x, r_bc, r_dt, r_decay, pack_list, resp_len, resp_prompt, d_skip
):
    head_count = p_dt.shape[1]
    groups = lax.axis_size("seq")
    block_heads = head_count // groups
    p_out, own_seed = prompt_part(p_x, p_bc, p_dt, p_decay, d_skip)
    own_seed, r_x, r_bc, r_dt, r_decay = lax.optimization_barrier(
        (own_seed, r_x, r_bc, r_dt, r_decay)
    )
    row_slot, owners = slot_layout(pack_list[0], resp_len, resp_prompt, r_x.shape[0])
    gathered_piece = gather_all(own_seed, "grp", (4, 2, 2, 2, 2))
    chosen = (owners[:, None] == jnp.arange(gathered_piece.shape[0])[None, :]).astype(jnp.bfloat16)
    slot_seeds = product("km,mhnp->khnp", chosen, gathered_piece).astype(jnp.bfloat16)
    skip_block = lax.dynamic_slice_in_dim(
        d_skip, lax.axis_index("seq") * block_heads, block_heads, 0
    )
    r_out = response_part(skip_block, r_x, r_bc, r_dt, r_decay, row_slot, slot_seeds)
    return (p_out, r_out)


def solution(mesh):
    placed = (
        P("grp", "seq", None),
        P("grp", "seq", None),
        P("grp", None, "seq"),
        P("grp", None, "seq"),
        P("grp", "seq"),
        P("grp", None),
        P("seq", "grp"),
        P("seq", "grp"),
        P("grp", None),
        P(),
        P(),
        P(),
    )
    return jax.shard_map(
        on_device,
        mesh=mesh,
        in_specs=placed,
        out_specs=(P("grp", "seq", None), P("grp", "seq")),
        check_vma=False,
    )
```
